32 devices in a mesh: py: 4 (over z), pz: 8 (over y, x, core).
Axes of the slice: x: 2, y: 2, z: 4, core: 2. Of those that a mesh axis runs over, the one named last changes fastest.
Arguments:
- start: float32 [32, 64, 512], P('py', 'pz'), may hold values from -36 to 36
- coef_x: float32 [32, 64, 512], P('py', 'pz'), may hold values from 0.5 to 2
- coef_y: float32 [32, 64, 512], P('py', 'pz'), may hold values from 0.5 to 2
- coef_z: float32 [32, 64, 512], P('py', 'pz'), may hold values from 0.5 to 2
- shifts: float32 [8], replicated, may hold values from 0 to 14
Outputs:
- orthonormal: float32 [9, 32, 64, 512], P(None, 'py', 'pz')
- triangle: float32 [9, 9], replicated
The draws below stay inside these ranges and needn't reach their ends.
All inputs are finite; a program needn't handle non-finite values.
Results may differ from the reference program's by a relative error of at most 0.0003.
Values sent between devices are 32-bit elements; how exact they have to be, the bound alone decides.
A program may use at most 128 MiB of HBM per device.

```python
import math
import jax
import jax.numpy as jnp
from jax import lax

NX = 512
S = 8
BASIS = 9
NY = 32
NZ = 64


def draw_start(key, part):
    first, second = jax.random.split(jax.random.fold_in(key, 11))
    shape = (NY, NZ, NX)
    spread = jnp.exp(jax.random.uniform(first, shape, jnp.float32, 0.0, math.log(10.0)))
    trend_y = 1.0 + 2.0 * jnp.arange(NY, dtype=jnp.float32) / max(NY - 1, 1)
    trend_z = 1.0 + 2.0 * jnp.arange(NZ, dtype=jnp.float32) / max(NZ - 1, 1)
    trend = trend_y[:, None, None] * trend_z[None, :, None]
    base = jnp.clip(jax.random.normal(second, shape, jnp.float32), -4.0, 4.0)
    return (base * spread * trend * 0.1).astype(jnp.float32)


def draw_shifts(key, part):
    order = jnp.arange(S, dtype=jnp.int32)
    flipped = (order & 1) << 2 | order & 2 | order >> 2 & 1
    nodes = 7.0 + 6.0 * jnp.cos(math.pi * (2.0 * flipped.astype(jnp.float32) + 1.0) / (2.0 * S))
    jitter = jax.random.uniform(jax.random.fold_in(key, 23), (S,), jnp.float32, -1.0, 1.0)
    return (nodes + jitter).astype(jnp.float32)


def levels(own_key, extent, pieces, smallest, largest):
    level, own = 1.0, jax.random.fold_in(own_key, 6)
    for axis_at, shards_of in pieces:
        draws = jnp.exp(jax.random.uniform(jax.random.fold_in(own, axis_at), (shards_of,), jnp.float32, smallest / len(pieces), largest / len(pieces)))
        level = level * jnp.repeat(draws, extent[axis_at] // shards_of).reshape([-1 if axis == axis_at else 1 for axis in range(len(extent))])
    return level


def setup_inputs(seed: int = 0) -> dict:
    splits = jax.random.split(jax.random.key(seed), 6)
    return {
        "start": draw_start(jax.random.fold_in(splits[5], 71), 0),
        "coef_x": jnp.clip(jnp.exp(math.log(2.0) - 1.3862944 * jax.random.uniform(splits[1], (NY, NZ, NX), jnp.float32) ** levels(splits[1], (NY, NZ, NX), ((0, 4), (1, 8)), -0.2, 0.2)), 0.5, 2.0),
        "coef_y": jnp.clip(jnp.exp(math.log(2.0) - 1.3862944 * jax.random.uniform(splits[2], (NY, NZ, NX), jnp.float32) ** levels(splits[2], (NY, NZ, NX), ((0, 4), (1, 8)), -0.2, 0.2)), 0.5, 2.0),
        "coef_z": jnp.clip(jnp.exp(math.log(2.0) - 1.3862944 * jax.random.uniform(splits[3], (NY, NZ, NX), jnp.float32) ** levels(splits[3], (NY, NZ, NX), ((0, 4), (1, 8)), -0.2, 0.2)), 0.5, 2.0),
        "shifts": draw_shifts(jax.random.fold_in(splits[5], 71), 0),
    }


def below_cells(array, dim):
    edge = jnp.zeros_like(lax.slice_in_dim(array, 0, 1, axis=dim))
    return jnp.concatenate([edge, lax.slice_in_dim(array, 0, array.shape[dim] - 1, axis=dim)], axis=dim)

def above_cells(array, dim):
    edge = jnp.zeros_like(lax.slice_in_dim(array, 0, 1, axis=dim))
    return jnp.concatenate([lax.slice_in_dim(array, 1, array.shape[dim], axis=dim), edge], axis=dim)

def operate(field, coef_x, coef_y, coef_z):
    result = jnp.zeros_like(field)
    for dim, coef in ((2, coef_x), (0, coef_y), (1, coef_z)):
        result = result + coef * (field - above_cells(field, dim))
        result = result + below_cells(coef, dim) * (field - below_cells(field, dim))
    return result

def forward(factor, vectors):
    count = factor.shape[0]
    solved = []
    for row in range(count):
        partial_sum = vectors[row]
        for inner in range(row):
            partial_sum = partial_sum - factor[inner, row] * solved[inner]
        solved.append(partial_sum / factor[row, row])
    return jnp.stack(solved)

def reference(start, coef_x, coef_y, coef_z, shifts):
    vectors = [start]
    current = start
    for level in range(S):
        image = operate(current, coef_x, coef_y, coef_z)
        current = (image - shifts[level] * current) * 0.125
        vectors.append(current)
    basis = jnp.stack(vectors)
    flat = basis.reshape(BASIS, NY, NZ * NX)

    def block_factor(index_y):
        tall = lax.dynamic_index_in_dim(flat, index_y, axis=1, keepdims=False).T
        return jnp.linalg.qr(tall, mode='r')
    blocks = lax.map(block_factor, jnp.arange(NY, dtype=jnp.int32))
    upper = jnp.linalg.qr(blocks.reshape(NY * BASIS, BASIS), mode='r')
    signs = jnp.where(jnp.diagonal(upper) >= 0, 1.0, -1.0).astype(upper.dtype)
    triangle = upper * signs[:, None] / math.sqrt(NX * NY * NZ)
    orthonormal = forward(triangle, basis.reshape(BASIS, -1)).reshape(basis.shape)
    return (orthonormal, triangle)
```

```python
import functools
import math

import jax
import jax.numpy as jnp
from jax import lax
from jax.experimental import pallas as pl
from jax.experimental.pallas import tpu as pltpu
from jax.sharding import PartitionSpec as P

step_scale = 0.125
MESH = pl.DeviceIdType.MESH
LANES = 128
SUBLANES = 8
Y_UP, Y_DOWN, Z_UP, Z_DOWN = range(4)


def two_sum(a, b):
    total = a + b
    virtual = total - a
    return total, (a - (total - virtual)) + (b - virtual)


def split(a):
    scaled = a * 4097.0
    high = scaled - (scaled - a)
    return high, a - high


def two_product(a, b):
    product = a * b
    a_high, a_low = split(a)
    b_high, b_low = split(b)
    error = ((a_high * b_high - product) + a_high * b_low + a_low * b_high) + a_low * b_low
    return product, error


def pair_add(a, b):
    total, error = two_sum(a[0], b[0])
    return total, error + (a[1] + b[1])


def renormal(a):
    total = a[0] + a[1]
    return total, a[1] - (total - a[0])


def tree(parts):
    while len(parts) > 1:
        rest = parts[len(parts) // 2 * 2 :]
        parts = [pair_add(parts[i], parts[i + 1]) for i in range(0, len(parts) - 1, 2)] + rest
    return parts[0]


def kernel(
    count_y,
    count_z,
    root_cells,
    start,
    coef_x,
    coef_y,
    coef_z,
    shifts,
    out,
    triangle,
    basis,
    high,
    low,
    packed,
    halo,
    coef_pack,
    coef_halo,
    partial,
    gram,
    gather_z,
    gather_y,
    splat,
    send_sem,
    recv_sem,
    coef_send,
    coef_recv,
    z_send,
    z_recv,
    y_send,
    y_recv,
):
    rows_y, rows_z, length = start.shape
    depth = shifts.shape[0]
    count = depth + 1
    padded = gram.shape[0] // 2
    me_y, me_z = lax.axis_index("py"), lax.axis_index("pz")

    barrier = pltpu.get_barrier_semaphore()
    for away in range(1, count_z):
        pl.semaphore_signal(
            barrier, inc=1, device_id={"pz": lax.rem(me_z + away, count_z)}, device_id_type=MESH
        )
    for away in range(1, count_y):
        pl.semaphore_signal(
            barrier, inc=1, device_id={"py": lax.rem(me_y + away, count_y)}, device_id_type=MESH
        )

    partial[...] = jnp.zeros_like(partial)
    has = {
        Y_UP: me_y < count_y - 1,
        Y_DOWN: me_y > 0,
        Z_UP: me_z < count_z - 1,
        Z_DOWN: me_z > 0,
    }
    comes = {Y_UP: has[Y_DOWN], Y_DOWN: has[Y_UP], Z_UP: has[Z_DOWN], Z_DOWN: has[Z_UP]}
    target = {
        Y_UP: {"py": me_y + 1},
        Y_DOWN: {"py": me_y - 1},
        Z_UP: {"pz": me_z + 1},
        Z_DOWN: {"pz": me_z - 1},
    }

    def pack(value_row, y, slot):
        packed[0, slot, pl.ds(y, 1), :] = value_row[rows_z - 1 : rows_z, :]
        packed[1, slot, pl.ds(y, 1), :] = value_row[0:1, :]

    def keep(value_row, y, slot):
        basis[slot, y] = value_row
        value_high, value_low = split(value_row)
        high[slot, y] = value_high
        low[slot, y] = value_low

    for y in range(rows_y):
        row = start[y]
        keep(row, y, 0)
        pack(row, y, 0)
        coef_pack[pl.ds(y, 1), :] = coef_z[y, rows_z - 1 : rows_z, :]

    for way in range(4):

        @pl.when(jnp.logical_not(comes[way]))
        def _():
            halo[way] = jnp.zeros_like(halo[way])
            if way in (Y_UP, Z_UP):
                coef_halo[way // 2] = jnp.zeros_like(coef_halo[way // 2])

    pl.semaphore_wait(barrier, count_z + count_y - 2)

    def halo_copy(way, slot):
        source = {
            Y_UP: basis.at[slot, rows_y - 1],
            Y_DOWN: basis.at[slot, 0],
            Z_UP: packed.at[0, slot],
            Z_DOWN: packed.at[1, slot],
        }[way]
        return pltpu.make_async_remote_copy(
            src_ref=source,
            dst_ref=halo.at[way, slot],
            send_sem=send_sem.at[way, slot],
            recv_sem=recv_sem.at[way, slot],
            device_id=target[way],
            device_id_type=MESH,
        )

    def coef_copy(way):
        return pltpu.make_async_remote_copy(
            src_ref=coef_y.at[rows_y - 1] if way == Y_UP else coef_pack,
            dst_ref=coef_halo.at[way // 2],
            send_sem=coef_send.at[way // 2],
            recv_sem=coef_recv.at[way // 2],
            device_id=target[way],
            device_id_type=MESH,
        )

    for way in (Y_UP, Z_UP):
        pl.when(has[way])(lambda way=way: coef_copy(way).start())

    lane = lax.broadcasted_iota(jnp.int32, (rows_z, length), 1)
    sub = lax.broadcasted_iota(jnp.int32, (rows_z, length), 0)
    square_sub = lax.broadcasted_iota(jnp.int32, (padded, LANES), 0)
    square_lane = lax.broadcasted_iota(jnp.int32, (padded, LANES), 1)

    def gram_column(column, g_high, g_low):
        def pair(i, carry):
            total = None
            for y in range(rows_y):
                a_high, a_low = high[i, y], low[i, y]
                b_high, b_low = high[column, y], low[column, y]
                lead = a_high * b_high
                minor = (a_high * b_low + a_low * b_high) + a_low * b_low
                if total is None:
                    total = (lead, minor)
                else:
                    total = pair_add(total, (lead, minor))
            chunks = [
                (total[0][:, x : x + LANES], total[1][:, x : x + LANES])
                for x in range(0, length, LANES)
            ]
            s, e = tree(chunks)
            at = pl.multiple_of(i * SUBLANES, SUBLANES)
            partial[0, pl.ds(at, SUBLANES), :] = s
            partial[1, pl.ds(at, SUBLANES), :] = e
            return carry

        lax.fori_loop(0, column + 1, pair, 0)
        parts = [
            (
                partial[0, pl.ds(s, padded, stride=SUBLANES), :],
                partial[1, pl.ds(s, padded, stride=SUBLANES), :],
            )
            for s in range(SUBLANES)
        ]
        total = tree(parts)
        shift = LANES // 2
        while shift:
            total = pair_add(
                total, (pltpu.roll(total[0], shift, 1), pltpu.roll(total[1], shift, 1))
            )
            shift //= 2
        total = renormal(total)
        eye = square_sub == square_lane
        in_column = jnp.logical_and(square_lane == column, square_sub <= column)
        in_row = jnp.logical_and(square_sub == column, square_lane <= column)
        result = []
        for g, piece in ((g_high, total[0]), (g_low, total[1])):
            row = jnp.sum(jnp.where(eye, piece, 0.0), axis=0, keepdims=True)
            g = jnp.where(in_column, piece, g)
            g = jnp.where(in_row, row, g)
            result.append(g)
        return result

    def level(slot, grams):
        for way in range(4):
            pl.when(has[way])(lambda way=way: halo_copy(way, slot).start())
        grams = gram_column(slot, *grams)

        @pl.when(slot == 0)
        def _():
            for way in (Y_UP, Z_UP):
                pl.when(has[way])(lambda way=way: coef_copy(way).wait_send())
                pl.when(comes[way])(lambda way=way: coef_copy(way).wait_recv())

        for way in range(4):
            pl.when(has[way])(lambda way=way: halo_copy(way, slot).wait_send())
            pl.when(comes[way])(lambda way=way: halo_copy(way, slot).wait_recv())

        shift = shifts[slot]
        below_z = coef_halo[1] * (halo[Z_UP, slot] - packed[1, slot])
        flux_low = coef_halo[0] * (halo[Y_UP, slot] - basis[slot, 0])
        for y in range(rows_y):
            row = basis[slot, y]
            ahead = jnp.where(lane == length - 1, 0.0, pltpu.roll(row, length - 1, 1))
            flux_x = coef_x[y] * (row - ahead)
            image = flux_x - jnp.where(lane == 0, 0.0, pltpu.roll(flux_x, 1, 1))
            above = halo[Y_DOWN, slot] if y == rows_y - 1 else basis[slot, y + 1]
            flux_y = coef_y[y] * (row - above)
            image = image + flux_y
            image = image - flux_low
            flux_low = flux_y
            up = jnp.where(
                sub == rows_z - 1,
                halo[Z_DOWN, slot, pl.ds(y, 1), :],
                pltpu.roll(row, rows_z - 1, 0),
            )
            flux_z = coef_z[y] * (row - up)
            image = image + flux_z
            image = image - jnp.where(sub == 0, below_z[y : y + 1, :], pltpu.roll(flux_z, 1, 0))
            fresh = (image - shift * row) * step_scale
            keep(fresh, y, slot + 1)
            pack(fresh, y, slot + 1)
        return grams

    zero = jnp.zeros((padded, LANES), jnp.float32)
    grams = lax.fori_loop(0, depth, level, [zero, zero])
    g_high, g_low = gram_column(depth, *grams)

    def total_over(g, me, size, axis, buffer, sends, recvs):
        buffer[me] = gram[...]
        copies = []
        for away in range(1, size):
            copies.append(
                pltpu.make_async_remote_copy(
                    src_ref=gram,
                    dst_ref=buffer.at[me],
                    send_sem=sends.at[away - 1],
                    recv_sem=recvs.at[away - 1],
                    device_id={axis: lax.rem(me + away, size)},
                    device_id_type=MESH,
                )
            )
        for copy in copies:
            copy.start()
        for copy in copies:
            copy.wait()
        return renormal(
            tree([(buffer[i, :padded], buffer[i, padded:]) for i in range(size)])
        )

    gram[:padded] = g_high
    gram[padded:] = g_low
    g_high, g_low = total_over(gram, me_z, count_z, "pz", gather_z, z_send, z_recv)
    gram[:padded] = g_high
    gram[padded:] = g_low
    g_high, g_low = total_over(gram, me_y, count_y, "py", gather_y, y_send, y_recv)

    tri = zero
    row_lane = lax.broadcasted_iota(jnp.int32, (1, LANES), 1)
    for k in range(count):
        row_high, row_low = g_high[k : k + 1, :], g_low[k : k + 1, :]
        d_high = jnp.broadcast_to(row_high[:, k : k + 1], (1, LANES))
        d_low = jnp.broadcast_to(row_low[:, k : k + 1], (1, LANES))
        factor = jnp.where(row_lane >= k, row_high / jnp.sqrt(d_high) / root_cells, 0.0)
        tri = jnp.where(square_sub == k, factor, tri)
        unit = 1.0 / jnp.broadcast_to(factor[:, k : k + 1], (SUBLANES, LANES))
        splat[k * count + k] = unit
        for i in range(k + 1, count):
            splat[k * count + i] = jnp.broadcast_to(factor[:, i : i + 1], (SUBLANES, LANES))
        if k == count - 1:
            break
        inverse = 1.0 / d_high
        lead = row_high * inverse
        product, error = two_product(lead, d_high)
        minor = (((row_high - product) - error) + (row_low - lead * d_low)) * inverse
        col_high = jnp.broadcast_to(g_high[:, k : k + 1], (padded, LANES))
        col_low = jnp.broadcast_to(g_low[:, k : k + 1], (padded, LANES))
        lead = jnp.broadcast_to(lead, (padded, LANES))
        minor = jnp.broadcast_to(minor, (padded, LANES))
        product, error = two_product(col_high, lead)
        error = error + (col_high * minor + col_low * lead)
        total, rest = two_sum(g_high, -product)
        g_high, g_low = renormal((total, rest + (g_low - error)))
    triangle[...] = tri[:count, :count]

    def substitute(y, carry):
        for x in range(0, length, LANES):
            solved = []
            for i in range(count):
                value = basis[i, y, :, x : x + LANES]
                for k in range(i):
                    value = value - splat[k * count + i] * solved[k]
                value = value * splat[i * count + i]
                out[i, y, :, x : x + LANES] = value
                solved.append(value)
        return carry

    lax.fori_loop(0, rows_y, substitute, 0)


def on_device(start, coef_x, coef_y, coef_z, shifts):
    rows_y, rows_z, length = start.shape
    depth = shifts.shape[0]
    count = depth + 1
    padded = (count + SUBLANES - 1) // SUBLANES * SUBLANES
    count_y, count_z = lax.axis_size("py"), lax.axis_size("pz")
    cells = length * rows_y * rows_z * count_y * count_z
    whole = pl.BlockSpec(memory_space=pltpu.VMEM)
    face = (rows_z, length)
    pltpu_f32 = lambda *shape: pltpu.VMEM(shape, jnp.float32)
    dma = pltpu.SemaphoreType.DMA
    return pl.pallas_call(
        functools.partial(kernel, count_y, count_z, math.sqrt(cells)),
        out_shape=(
            jax.ShapeDtypeStruct((count, rows_y, rows_z, length), jnp.float32),
            jax.ShapeDtypeStruct((count, count), jnp.float32),
        ),
        in_specs=[whole] * 4 + [pl.BlockSpec(memory_space=pltpu.SMEM)],
        out_specs=(whole, whole),
        scratch_shapes=[
            pltpu_f32(count, rows_y, rows_z, length),
            pltpu_f32(count, rows_y, rows_z, length),
            pltpu_f32(count, rows_y, rows_z, length),
            pltpu_f32(2, count, rows_y, length),
            pltpu_f32(4, depth, *face),
            pltpu_f32(rows_y, length),
            pltpu_f32(2, *face),
            pltpu_f32(2, padded * SUBLANES, LANES),
            pltpu_f32(2 * padded, LANES),
            pltpu_f32(count_z, 2 * padded, LANES),
            pltpu_f32(count_y, 2 * padded, LANES),
            pltpu_f32(count * count, SUBLANES, LANES),
            dma((4, depth)),
            dma((4, depth)),
            dma((2,)),
            dma((2,)),
            dma((count_z - 1,)),
            dma((count_z - 1,)),
            dma((count_y - 1,)),
            dma((count_y - 1,)),
        ],
        compiler_params=pltpu.CompilerParams(collective_id=0, has_side_effects=True),
    )(start, coef_x, coef_y, coef_z, shifts)


def solution(mesh):
    placed = (
        P("py", "pz", None),
        P("py", "pz", None),
        P("py", "pz", None),
        P("py", "pz", None),
        P(),
    )
    return jax.shard_map(
        on_device,
        mesh=mesh,
        in_specs=placed,
        out_specs=(P(None, "py", "pz", None), P()),
        check_vma=False,
    )
```

```python
import functools
import math

import jax
import jax.numpy as jnp
from jax import lax
from jax.experimental import pallas as pl
from jax.experimental.pallas import tpu as pltpu
from jax.sharding import PartitionSpec as P

step_scale = 0.125
MESH = pl.DeviceIdType.MESH
LANES = 128
SUBLANES = 8
Y_UP, Y_DOWN, Z_UP, Z_DOWN = range(4)


def two_sum(a, b):
    total = a + b
    virtual = total - a
    return total, (a - (total - virtual)) + (b - virtual)


def split(a):
    scaled = a * 4097.0
    high = scaled - (scaled - a)
    return high, a - high


def two_product(a, b):
    product = a * b
    a_high, a_low = split(a)
    b_high, b_low = split(b)
    error = ((a_high * b_high - product) + a_high * b_low + a_low * b_high) + a_low * b_low
    return product, error


def pair_add(a, b):
    total, error = two_sum(a[0], b[0])
    return total, error + (a[1] + b[1])


def renormal(a):
    total = a[0] + a[1]
    return total, a[1] - (total - a[0])


def tree(parts):
    while len(parts) > 1:
        rest = parts[len(parts) // 2 * 2 :]
        parts = [pair_add(parts[i], parts[i + 1]) for i in range(0, len(parts) - 1, 2)] + rest
    return parts[0]


def wrap(high, low):
    lane = lax.broadcasted_iota(jnp.int32, high.shape, 1)
    return jnp.where(lane < LANES // 2, high, pltpu.roll(low, LANES // 2, 1))


def unwrapped_sum(buffer):
    parts = []
    for i in range(buffer.shape[0]):
        value = buffer[i]
        parts.append((value, pltpu.roll(value, LANES // 2, 1)))
    total = renormal(tree(parts))
    lane = lax.broadcasted_iota(jnp.int32, total[0].shape, 1)
    return [jnp.where(lane < LANES // 2, piece, 0.0) for piece in total]


def kernel(
    count_y,
    count_z,
    root_cells,
    start_hbm,
    x_hbm,
    y_hbm,
    z_hbm,
    shifts,
    basis_hbm,
    triangle,
    basis,
    high,
    low,
    coef_x,
    coef_y,
    coef_z,
    packed,
    halo,
    coef_pack,
    coef_halo,
    partial,
    early_source,
    early_z,
    early_y,
    last_source,
    last_z,
    last_y,
    load_sem,
    store_sem,
    send_sem,
    recv_sem,
    coef_send,
    coef_recv,
    z_send,
    z_recv,
    y_send,
    y_recv,
):
    depth = shifts.shape[0]
    count = depth + 1
    rows_y, rows_z, length = coef_x.shape
    padded = triangle.shape[0]
    me_y, me_z = lax.axis_index("py"), lax.axis_index("pz")

    barrier = pltpu.get_barrier_semaphore()
    for away in range(1, count_z):
        pl.semaphore_signal(
            barrier, inc=1, device_id={"pz": lax.rem(me_z + away, count_z)}, device_id_type=MESH
        )
    for away in range(1, count_y):
        pl.semaphore_signal(
            barrier, inc=1, device_id={"py": lax.rem(me_y + away, count_y)}, device_id_type=MESH
        )

    loads = [
        pltpu.make_async_copy(source, target, load_sem.at[i])
        for i, (source, target) in enumerate(
            (
                (start_hbm, basis.at[0]),
                (z_hbm, coef_z),
                (y_hbm, coef_y),
                (x_hbm, coef_x),
            )
        )
    ]
    for load in loads:
        load.start()
    partial[...] = jnp.zeros_like(partial)
    has = {
        Y_UP: me_y < count_y - 1,
        Y_DOWN: me_y > 0,
        Z_UP: me_z < count_z - 1,
        Z_DOWN: me_z > 0,
    }
    comes = {Y_UP: has[Y_DOWN], Y_DOWN: has[Y_UP], Z_UP: has[Z_DOWN], Z_DOWN: has[Z_UP]}
    target = {
        Y_UP: {"py": me_y + 1},
        Y_DOWN: {"py": me_y - 1},
        Z_UP: {"pz": me_z + 1},
        Z_DOWN: {"pz": me_z - 1},
    }

    def pack(value_row, y, slot):
        packed[0, slot, pl.ds(y, 1), :] = value_row[rows_z - 1 : rows_z, :]
        packed[1, slot, pl.ds(y, 1), :] = value_row[0:1, :]

    def keep(value_row, y, slot):
        value_high, value_low = split(value_row)
        high[slot, y] = value_high
        low[slot, y] = value_low

    for way in range(4):

        @pl.when(jnp.logical_not(comes[way]))
        def _():
            halo[way] = jnp.zeros_like(halo[way])
            if way in (Y_UP, Z_UP):
                coef_halo[way // 2] = jnp.zeros_like(coef_halo[way // 2])

    loads[0].wait()
    loads[1].wait()
    for y in range(rows_y):
        row = basis[0, y]
        keep(row, y, 0)
        pack(row, y, 0)
        coef_pack[pl.ds(y, 1), :] = coef_z[y, rows_z - 1 : rows_z, :]
    loads[2].wait()
    pl.semaphore_wait(barrier, count_z + count_y - 2)

    def halo_copy(way, slot):
        source = {
            Y_UP: basis.at[slot, rows_y - 1],
            Y_DOWN: basis.at[slot, 0],
            Z_UP: packed.at[0, slot],
            Z_DOWN: packed.at[1, slot],
        }[way]
        return pltpu.make_async_remote_copy(
            src_ref=source,
            dst_ref=halo.at[way, slot],
            send_sem=send_sem.at[way, slot],
            recv_sem=recv_sem.at[way, slot],
            device_id=target[way],
            device_id_type=MESH,
        )

    def coef_copy(way):
        return pltpu.make_async_remote_copy(
            src_ref=coef_y.at[rows_y - 1] if way == Y_UP else coef_pack,
            dst_ref=coef_halo.at[way // 2],
            send_sem=coef_send.at[way // 2],
            recv_sem=coef_recv.at[way // 2],
            device_id=target[way],
            device_id_type=MESH,
        )

    lane = lax.broadcasted_iota(jnp.int32, (rows_z, length), 1)
    sub = lax.broadcasted_iota(jnp.int32, (rows_z, length), 0)
    square_sub = lax.broadcasted_iota(jnp.int32, (padded, LANES), 0)
    square_lane = lax.broadcasted_iota(jnp.int32, (padded, LANES), 1)

    def gram_column(column, g_high, g_low):
        def pair(i, carry):
            total = None
            for y in range(rows_y):
                a_high, a_low = high[i, y], low[i, y]
                b_high, b_low = high[column, y], low[column, y]
                lead = a_high * b_high
                minor = (a_high * b_low + a_low * b_high) + a_low * b_low
                if total is None:
                    total = (lead, minor)
                else:
                    total = pair_add(total, (lead, minor))
            chunks = [
                (total[0][:, x : x + LANES], total[1][:, x : x + LANES])
                for x in range(0, length, LANES)
            ]
            s, e = tree(chunks)
            at = pl.multiple_of(i * SUBLANES, SUBLANES)
            partial[0, pl.ds(at, SUBLANES), :] = s
            partial[1, pl.ds(at, SUBLANES), :] = e
            return carry

        lax.fori_loop(0, column + 1, pair, 0)
        parts = [
            (
                partial[0, pl.ds(s, padded, stride=SUBLANES), :],
                partial[1, pl.ds(s, padded, stride=SUBLANES), :],
            )
            for s in range(SUBLANES)
        ]
        total = tree(parts)
        shift = LANES // 2
        while shift:
            total = pair_add(
                total, (pltpu.roll(total[0], shift, 1), pltpu.roll(total[1], shift, 1))
            )
            shift //= 2
        total = renormal(total)
        eye = square_sub == square_lane
        in_column = jnp.logical_and(square_lane == column, square_sub <= column)
        in_row = jnp.logical_and(square_sub == column, square_lane <= column)
        result = []
        for g, piece in ((g_high, total[0]), (g_low, total[1])):
            row = jnp.sum(jnp.where(eye, piece, 0.0), axis=0, keepdims=True)
            g = jnp.where(in_column, piece, g)
            g = jnp.where(in_row, row, g)
            result.append(g)
        return result

    def store(slot):
        return pltpu.make_async_copy(basis.at[slot], basis_hbm.at[slot], store_sem.at[slot])

    def exchange(source, buffer, me, size, axis, sends, recvs, stage):
        return [
            pltpu.make_async_remote_copy(
                src_ref=source,
                dst_ref=buffer.at[me],
                send_sem=sends.at[stage, away - 1],
                recv_sem=recvs.at[stage, away - 1],
                device_id={axis: lax.rem(me + away, size)},
                device_id_type=MESH,
            )
            for away in range(1, size)
        ]

    def begin(copies, source, buffer, me, value):
        source[...] = value
        buffer[me] = value
        for copy in copies:
            copy.start()

    def end(copies, buffer):
        for copy in copies:
            copy.wait()
        return unwrapped_sum(buffer)

    early_z_copies = exchange(early_source.at[0], early_z, me_z, count_z, "pz", z_send, z_recv, 0)
    early_y_copies = exchange(early_source.at[1], early_y, me_y, count_y, "py", y_send, y_recv, 0)
    last_z_copies = exchange(last_source.at[0], last_z, me_z, count_z, "pz", z_send, z_recv, 1)
    last_y_copies = exchange(last_source.at[1], last_y, me_y, count_y, "py", y_send, y_recv, 1)

    def level(slot, grams, first=False, hook=None):
        for way in range(4):
            pl.when(has[way])(lambda way=way: halo_copy(way, slot).start())
        if first:
            for way in (Y_UP, Z_UP):
                pl.when(has[way])(lambda way=way: coef_copy(way).start())
        store(slot).start()
        grams = gram_column(slot, *grams)
        if hook is not None:
            hook(grams)
        if first:
            loads[3].wait()
            for way in (Y_UP, Z_UP):
                pl.when(has[way])(lambda way=way: coef_copy(way).wait_send())
                pl.when(comes[way])(lambda way=way: coef_copy(way).wait_recv())

        for way in range(4):
            pl.when(has[way])(lambda way=way: halo_copy(way, slot).wait_send())
            pl.when(comes[way])(lambda way=way: halo_copy(way, slot).wait_recv())

        shift = shifts[slot]
        below_z = coef_halo[1] * (halo[Z_UP, slot] - packed[1, slot])
        flux_low = coef_halo[0] * (halo[Y_UP, slot] - basis[slot, 0])
        for y in range(rows_y):
            row = basis[slot, y]
            ahead = jnp.where(lane == length - 1, 0.0, pltpu.roll(row, length - 1, 1))
            flux_x = coef_x[y] * (row - ahead)
            image = flux_x - jnp.where(lane == 0, 0.0, pltpu.roll(flux_x, 1, 1))
            above = halo[Y_DOWN, slot] if y == rows_y - 1 else basis[slot, y + 1]
            flux_y = coef_y[y] * (row - above)
            image = image + flux_y
            image = image - flux_low
            flux_low = flux_y
            up = jnp.where(
                sub == rows_z - 1,
                halo[Z_DOWN, slot, pl.ds(y, 1), :],
                pltpu.roll(row, rows_z - 1, 0),
            )
            flux_z = coef_z[y] * (row - up)
            image = image + flux_z
            image = image - jnp.where(sub == 0, below_z[y : y + 1, :], pltpu.roll(flux_z, 1, 0))
            fresh = (image - shift * row) * step_scale
            basis[slot + 1, y] = fresh
            keep(fresh, y, slot + 1)
            pack(fresh, y, slot + 1)
        return grams

    def early_first(grams):
        begin(early_z_copies, early_source.at[0], early_z, me_z, wrap(*grams))

    def early_second(grams):
        total = end(early_z_copies, early_z)
        begin(early_y_copies, early_source.at[1], early_y, me_y, wrap(*total))

    zero = jnp.zeros((padded, LANES), jnp.float32)
    grams = level(0, [zero, zero], first=True)
    grams = lax.fori_loop(1, depth - 2, level, grams)
    grams = level(depth - 2, grams, hook=early_first)
    grams = level(depth - 1, grams, hook=early_second)
    store(depth).start()
    grams = gram_column(depth, *grams)

    tile_sub = lax.broadcasted_iota(jnp.int32, (SUBLANES, LANES), 0)
    tail = [
        jnp.where(tile_sub == 0, g[depth - 1 : depth, :], jnp.where(tile_sub == 1, g[depth:count, :], 0.0))
        for g in grams
    ]
    begin(last_z_copies, last_source.at[0], last_z, me_z, wrap(*tail))
    tail = end(last_z_copies, last_z)
    begin(last_y_copies, last_source.at[1], last_y, me_y, wrap(*tail))
    head = end(early_y_copies, early_y)
    tail = end(last_y_copies, last_y)
    eye = square_sub == square_lane
    grams = []
    for g, rows in zip(head, tail):
        for k, row in ((depth - 1, rows[0:1, :]), (depth, rows[1:2, :])):
            column = jnp.sum(jnp.where(eye, row, 0.0), axis=1, keepdims=True)
            g = jnp.where(square_lane == k, column, g)
            g = jnp.where(square_sub == k, row, g)
        grams.append(g)
    g_high, g_low = grams

    tri = zero
    row_lane = lax.broadcasted_iota(jnp.int32, (1, LANES), 1)
    for k in range(count):
        row_high, row_low = g_high[k : k + 1, :], g_low[k : k + 1, :]
        d_high = jnp.broadcast_to(row_high[:, k : k + 1], (1, LANES))
        d_low = jnp.broadcast_to(row_low[:, k : k + 1], (1, LANES))
        factor = jnp.where(row_lane >= k, row_high / jnp.sqrt(d_high) / root_cells, 0.0)
        tri = jnp.where(square_sub == k, factor, tri)
        if k == count - 1:
            break
        inverse = 1.0 / d_high
        lead = row_high * inverse
        product, error = two_product(lead, d_high)
        minor = (((row_high - product) - error) + (row_low - lead * d_low)) * inverse
        col_high = jnp.broadcast_to(g_high[:, k : k + 1], (padded, LANES))
        col_low = jnp.broadcast_to(g_low[:, k : k + 1], (padded, LANES))
        lead = jnp.broadcast_to(lead, (padded, LANES))
        minor = jnp.broadcast_to(minor, (padded, LANES))
        product, error = two_product(col_high, lead)
        error = error + (col_high * minor + col_low * lead)
        total, rest = two_sum(g_high, -product)
        g_high, g_low = renormal((total, rest + (g_low - error)))
    triangle[...] = tri
    for slot in range(count):
        store(slot).wait()


def substitute(basis, factor, out, triangle, splat):
    count, rows_y, rows_z, length = basis.shape

    @pl.when(pl.program_id(0) == 0)
    def _():
        tri = factor[...]
        triangle[...] = tri[:count, :count]
        for k in range(count):
            for i in range(k, count):
                value = jnp.broadcast_to(tri[k : k + 1, i : i + 1], (SUBLANES, LANES))
                splat[k * count + i] = 1.0 / value if i == k else value

    def plane(y, carry):
        for x in range(0, length, LANES):
            solved = []
            for i in range(count):
                value = basis[i, y, :, x : x + LANES]
                for k in range(i):
                    value = value - splat[k * count + i] * solved[k]
                value = value * splat[i * count + i]
                out[i, y, :, x : x + LANES] = value
                solved.append(value)
        return carry

    lax.fori_loop(0, rows_y, plane, 0)


def on_device(start, coef_x, coef_y, coef_z, shifts):
    rows_y, rows_z, length = start.shape
    depth = shifts.shape[0]
    count = depth + 1
    padded = (count + SUBLANES - 1) // SUBLANES * SUBLANES
    count_y, count_z = lax.axis_size("py"), lax.axis_size("pz")
    cells = length * rows_y * rows_z * count_y * count_z
    whole = pl.BlockSpec(memory_space=pltpu.VMEM)
    face = (rows_z, length)
    pltpu_f32 = lambda *shape: pltpu.VMEM(shape, jnp.float32)
    dma = pltpu.SemaphoreType.DMA
    anywhere = pl.BlockSpec(memory_space=pl.ANY)
    basis, factor = pl.pallas_call(
        functools.partial(kernel, count_y, count_z, math.sqrt(cells)),
        out_shape=(
            jax.ShapeDtypeStruct((count, rows_y, rows_z, length), jnp.float32),
            jax.ShapeDtypeStruct((padded, LANES), jnp.float32),
        ),
        in_specs=[anywhere] * 4 + [pl.BlockSpec(memory_space=pltpu.SMEM)],
        out_specs=(anywhere, whole),
        scratch_shapes=[
            pltpu_f32(count, rows_y, rows_z, length),
            pltpu_f32(count, rows_y, rows_z, length),
            pltpu_f32(count, rows_y, rows_z, length),
            pltpu_f32(rows_y, rows_z, length),
            pltpu_f32(rows_y, rows_z, length),
            pltpu_f32(rows_y, rows_z, length),
            pltpu_f32(2, count, rows_y, length),
            pltpu_f32(4, depth, *face),
            pltpu_f32(rows_y, length),
            pltpu_f32(2, *face),
            pltpu_f32(2, padded * SUBLANES, LANES),
            pltpu_f32(2, padded, LANES),
            pltpu_f32(count_z, padded, LANES),
            pltpu_f32(count_y, padded, LANES),
            pltpu_f32(2, SUBLANES, LANES),
            pltpu_f32(count_z, SUBLANES, LANES),
            pltpu_f32(count_y, SUBLANES, LANES),
            dma((4,)),
            dma((count,)),
            dma((4, depth)),
            dma((4, depth)),
            dma((2,)),
            dma((2,)),
            dma((2, count_z - 1)),
            dma((2, count_z - 1)),
            dma((2, count_y - 1)),
            dma((2, count_y - 1)),
        ],
        compiler_params=pltpu.CompilerParams(collective_id=0, has_side_effects=True),
    )(start, coef_x, coef_y, coef_z, shifts)
    block = (count, max(1, rows_y // 4), rows_z, length)
    planes = pl.BlockSpec(block, lambda i: (0, i, 0, 0))
    return pl.pallas_call(
        substitute,
        grid=(rows_y // block[1],),
        out_shape=(
            jax.ShapeDtypeStruct((count, rows_y, rows_z, length), jnp.float32),
            jax.ShapeDtypeStruct((count, count), jnp.float32),
        ),
        in_specs=[planes, pl.BlockSpec((padded, LANES), lambda i: (0, 0))],
        out_specs=(planes, pl.BlockSpec((count, count), lambda i: (0, 0))),
        scratch_shapes=[pltpu_f32(count * count, SUBLANES, LANES)],
    )(basis, factor)


def solution(mesh):
    placed = (
        P("py", "pz", None),
        P("py", "pz", None),
        P("py", "pz", None),
        P("py", "pz", None),
        P(),
    )
    return jax.shard_map(
        on_device,
        mesh=mesh,
        in_specs=placed,
        out_specs=(P(None, "py", "pz", None), P()),
        check_vma=False,
    )
```
